32 devices in a mesh: ctx: 8 (over z, x), tp: 4 (over y, core).
Axes of the slice: x: 2, y: 2, z: 4, core: 2. Of those that a mesh axis runs over, the one named last changes fastest.
Arguments:
- queries: bfloat16 [8192, 1024], P('tp', 'ctx'), may hold values from -6 to 6
- key_signal: bfloat16 [8192, 1024], P('tp', 'ctx'), may hold values from -6 to 6
- value_signal: bfloat16 [8192, 1024], P('tp', 'ctx'), may hold values from -6 to 6
- cotangent: bfloat16 [8192, 1024], P('tp', 'ctx'), may hold values from -6 to 6
- short_weight: float32 [3, 7, 8192], P(None, None, 'tp'), may hold values from -2 to 2
- residues: float32 [8192, 16], P('tp'), may hold values from -1.5 to 1.5
- decay_rates: float32 [8192, 16], P('tp'), may hold values from 0.0001 to 0.03
- skip_gain: float32 [8192], P('tp'), may hold values from 0.5 to 1.5
Outputs:
- mixed: bfloat16 [8192, 1024], P('tp', 'ctx')
- grad_queries: bfloat16 [8192, 1024], P('tp', 'ctx')
- grad_keys: bfloat16 [8192, 1024], P('tp', 'ctx')
- grad_values: bfloat16 [8192, 1024], P('tp', 'ctx')
- grad_short: float32 [3, 7, 8192], P(None, None, 'tp')
- grad_residues: float32 [8192, 16], P('tp')
- grad_skip: float32 [8192], P('tp')
The draws below stay inside these ranges and needn't reach their ends.
All inputs are finite; a program needn't handle non-finite values.
Results may differ from the reference program's by a relative error of at most 0.015.
Values may be sent and summed in bfloat16 or wider, within the bound.
A program may use at most 128 MiB of HBM per device.

```python
import math
import jax
import jax.numpy as jnp
from jax import lax

D = 8192
MODES = 16
KS = 7
SEQ = 1024


def block_scale(rng, shape, split, low, top_value):
    def one(dim, shards_of):
        draws = jax.random.uniform(jax.random.fold_in(jax.random.fold_in(rng, 6), dim), (shards_of,), jnp.float32, low / len(split), top_value / len(split))
        return jnp.repeat(jnp.exp(draws), shape[dim] // shards_of).reshape((-1,) + (1,) * (len(shape) - dim - 1))

    loudness = one(*split[0])
    for cut in split[1:]:
        loudness = loudness * one(*cut)
    return loudness


def gaussian(rng, extent, width, limit, pieces=(), kind=jnp.bfloat16):
    level = block_scale(rng, extent, pieces, -0.22, 0.18) if pieces else 1.0
    values = jax.random.normal(rng, extent, jnp.float32) * width * level
    return jnp.minimum(jnp.maximum(values, -limit), limit).astype(kind)


def setup_inputs(seed: int = 0) -> dict:
    seeds = jax.random.split(jax.random.key(seed), 9)
    queries = gaussian(seeds[0], (D, SEQ), 1.0, 6.0, ((0, 4), (1, 8)))
    key_signal = gaussian(seeds[1], (D, SEQ), 1.0, 6.0, ((0, 4), (1, 8)))
    value_signal = gaussian(seeds[2], (D, SEQ), 1.0, 6.0, ((0, 4), (1, 8)))
    cotangent = gaussian(seeds[3], (D, SEQ), 1.0, 6.0, ((0, 4), (1, 8)))
    short_weight = gaussian(seeds[4], (3, KS, D), KS ** -0.5, 2.0, ((2, 4),), jnp.float32)
    residues = gaussian(seeds[5], (D, MODES), 0.25, 1.5, ((0, 4),), jnp.float32)
    decay_rates = jnp.clip(jnp.exp(math.log(0.03) - 5.7037825 * jax.random.uniform(seeds[6], (D, MODES), jnp.float32) ** block_scale(seeds[6], (D, MODES), ((0, 4),), -0.2, 0.2)), 0.0001, 0.03)
    skip_gain = jnp.clip(0.5 + 1.0 * jax.random.uniform(seeds[7], (D,), jnp.float32) ** block_scale(seeds[7], (D,), ((0, 4),), -0.2, 0.2), 0.5, 1.5)
    return dict(queries=queries, key_signal=key_signal, value_signal=value_signal, cotangent=cotangent, short_weight=short_weight, residues=residues, decay_rates=decay_rates, skip_gain=skip_gain)


def causal_taps(signal, weight):
    margin = weight.shape[0] - 1
    length = signal.shape[1]
    padded = jnp.pad(signal, ((0, 0), (margin, 0)))
    total = jnp.zeros(signal.shape, jnp.float32)
    for tap_index in range(weight.shape[0]):
        total = total + weight[tap_index][:, None] * padded[:, margin - tap_index:margin - tap_index + length]
    return total

def anti_taps(signal, weight):
    margin = weight.shape[0] - 1
    length = signal.shape[1]
    padded = jnp.pad(signal, ((0, 0), (0, margin)))
    total = jnp.zeros(signal.shape, jnp.float32)
    for tap_index in range(weight.shape[0]):
        total = total + weight[tap_index][:, None] * padded[:, tap_index:tap_index + length]
    return total

def tap_grads(grads, signal, taps):
    margin = taps - 1
    length = signal.shape[1]
    padded = jnp.pad(signal, ((0, 0), (margin, 0)))
    rows_out = []
    for tap_index in range(taps):
        rows_out.append(lax.optimization_barrier(jnp.sum(grads * padded[:, margin - tap_index:margin - tap_index + length], axis=1)))
    return jnp.stack(rows_out, 0)

def block_terms(operands):
    queries, key_signal, value_signal, cotangent, weights, residues, decay_rates, skip_gain = operands
    weights = jnp.transpose(weights, (1, 2, 0))
    q_in = queries.astype(jnp.float32)
    k_in = key_signal.astype(jnp.float32)
    v_in = value_signal.astype(jnp.float32)
    q_short = causal_taps(q_in, weights[0]).astype(jnp.bfloat16)
    k_short = causal_taps(k_in, weights[1]).astype(jnp.bfloat16)
    v_short = causal_taps(v_in, weights[2]).astype(jnp.bfloat16)
    gated = (k_short.astype(jnp.float32) * v_short.astype(jnp.float32)).astype(jnp.bfloat16)
    lags = jnp.arange(SEQ).astype(jnp.float32)
    powers = jnp.exp(-decay_rates[:, :, None] * lags)
    gain = residues * jnp.sqrt(2.0 * decay_rates)
    filt = jnp.einsum('bm,bmt->bt', gain, powers)
    spec_z = jnp.fft.rfft(gated.astype(jnp.float32), n=2 * SEQ, axis=1)
    spec_h = jnp.fft.rfft(filt, n=2 * SEQ, axis=1)
    conv = jnp.fft.irfft(spec_z * spec_h, n=2 * SEQ, axis=1)[:, :SEQ].astype(jnp.bfloat16)
    mix = conv.astype(jnp.float32) + skip_gain[:, None] * gated.astype(jnp.float32)
    mixed = (q_short.astype(jnp.float32) * mix).astype(jnp.bfloat16)
    cot = cotangent.astype(jnp.float32)
    grad_mix = (cot * q_short.astype(jnp.float32)).astype(jnp.bfloat16)
    grad_qshort = (cot * mix).astype(jnp.bfloat16)
    spec_g = jnp.fft.rfft(grad_mix.astype(jnp.float32), n=2 * SEQ, axis=1)
    grad_conv = jnp.fft.irfft(spec_g * jnp.conj(spec_h), n=2 * SEQ, axis=1)[:, :SEQ].astype(jnp.bfloat16)
    grad_gated = grad_conv.astype(jnp.float32) + skip_gain[:, None] * grad_mix.astype(jnp.float32)
    grad_kshort = (grad_gated * v_short.astype(jnp.float32)).astype(jnp.bfloat16)
    grad_vshort = (grad_gated * k_short.astype(jnp.float32)).astype(jnp.bfloat16)
    grad_queries = anti_taps(grad_qshort.astype(jnp.float32), weights[0]).astype(jnp.bfloat16)
    grad_keys = anti_taps(grad_kshort.astype(jnp.float32), weights[1]).astype(jnp.bfloat16)
    grad_values = anti_taps(grad_vshort.astype(jnp.float32), weights[2]).astype(jnp.bfloat16)
    scale = SEQ ** (-0.5)
    grad_short = jnp.stack([tap_grads(grad_qshort.astype(jnp.float32), q_in, KS), tap_grads(grad_kshort.astype(jnp.float32), k_in, KS), tap_grads(grad_vshort.astype(jnp.float32), v_in, KS)], 0) * scale
    grad_skip = lax.optimization_barrier(jnp.sum(grad_mix.astype(jnp.float32) * gated.astype(jnp.float32), axis=1)) * scale
    lag_sums = jnp.fft.irfft(spec_g * jnp.conj(spec_z), n=2 * SEQ, axis=1)[:, :SEQ]
    grad_residues = jnp.sqrt(2.0 * decay_rates) * jnp.einsum('bt,bmt->bm', lag_sums, powers) * scale
    return (mixed, grad_queries, grad_keys, grad_values, grad_short, grad_residues, grad_skip)

def reference(queries, key_signal, value_signal, cotangent, short_weight, residues, decay_rates, skip_gain):
    block = min(D, 128)
    count = D // block
    weights = jnp.transpose(short_weight, (2, 0, 1)).reshape(count, block, 3, KS)
    results = lax.map(block_terms, (queries.reshape(count, block, SEQ), key_signal.reshape(count, block, SEQ), value_signal.reshape(count, block, SEQ), cotangent.reshape(count, block, SEQ), weights, residues.reshape(count, block, MODES), decay_rates.reshape(count, block, MODES), skip_gain.reshape(count, block)))
    mixed, grad_queries, grad_keys, grad_values, grad_short, grad_residues, grad_skip = results
    grad_short = jnp.transpose(grad_short, (1, 2, 0, 3)).reshape(3, KS, D)
    return (mixed.reshape(D, SEQ), grad_queries.reshape(D, SEQ), grad_keys.reshape(D, SEQ), grad_values.reshape(D, SEQ), grad_short, grad_residues.reshape(D, MODES), grad_skip.reshape(D))
```

```python
import functools
import math

import jax
import jax.numpy as jnp
import ml_dtypes
import numpy as np
from jax import lax
from jax.experimental import pallas as pl
from jax.experimental.pallas import tpu as pltpu
from jax.sharding import PartitionSpec as P

F32 = jnp.float32
BF16 = jnp.bfloat16
NODES = 16


def two(table):
    high = table.astype(ml_dtypes.bfloat16)
    low = (table - high.astype(np.float64)).astype(ml_dtypes.bfloat16)
    return high, low


@functools.lru_cache(None)
def tables(rows, modes):
    top = rows - 1
    half = [round(top / 2 - top / 2 * math.cos((2 * k + 1) * math.pi / (2 * NODES))) for k in range(NODES // 2)]
    nodes = np.array(half + [top - x for x in half[::-1]], np.float64)
    basis = np.ones((NODES, rows))
    spots = np.arange(rows, dtype=np.float64)
    for k in range(NODES):
        for other in range(NODES):
            if other != k:
                basis[k] *= (spots - nodes[other]) / (nodes[k] - nodes[other])
    spread = np.tile(basis, (modes, 1))
    back = spread[:, ::-1]
    omega = 2 * math.pi * (np.arange(rows) + 0.5) / (2 * rows)
    angle = spots[:, None] * omega[None, :]
    dft = np.concatenate([np.cos(angle), -np.sin(angle)], 1)
    inv = np.concatenate([np.cos(angle), -np.sin(angle)], 1).T / rows
    out = {}
    out["dft"] = np.concatenate(two(dft), 0)
    out["inv"] = np.concatenate(two(inv), 1)
    out["spec_hi"], out["spec_lo"] = two(spread @ dft)
    out["mom"] = np.concatenate(two(spread.T), 0)
    out["mom_back"] = np.concatenate(two(back.T), 0)
    out["lag_hi"], out["lag_lo"] = two(inv @ spread.T)
    out["out"] = np.concatenate(two(spread), 1)
    out["out_back"] = np.concatenate(two(back), 1)
    eye = np.eye(modes)
    out["times"] = np.kron(eye, nodes[None, :]).astype(ml_dtypes.bfloat16)
    pick = np.kron(eye, np.ones((1, NODES)))
    out["pick"] = pick.astype(ml_dtypes.bfloat16)
    return out


def mm(a, b):
    return lax.dot_general(a, b, (((1,), (0,)), ((), ())), preferred_element_type=F32)


def mm_nt(a, b):
    return lax.dot_general(a, b, (((1,), (1,)), ((), ())), preferred_element_type=F32)


def mm_tn(a, b):
    return lax.dot_general(a, b, (((0,), (0,)), ((), ())), preferred_element_type=F32)


def parts(x, count):
    out = []
    for _ in range(count):
        piece = x.astype(BF16)
        out.append(piece)
        x = x - piece.astype(F32)
    return out


def exact(op, x, table, count):
    total = None
    for piece in parts(x, count):
        term = op(piece, table)
        total = term if total is None else total + term
    return total


def powers_kernel(dec_ref, res_ref, times_ref, pick_ref, hi_ref, lo_ref, pow_ref, spec_ref):
    dec = dec_ref[...]
    gain = res_ref[...] * jnp.sqrt(2.0 * dec)
    powers = jnp.exp(-exact(mm, dec, times_ref[...], 3))
    pow_ref[...] = powers
    high, low = parts(powers * exact(mm, gain, pick_ref[...], 3), 2)
    spec_ref[...] = mm(high, hi_ref[...]) + mm(low, hi_ref[...]) + mm(high, lo_ref[...])


def shifted(x, halo, lane, j):
    rows = x.shape[1]
    if j == 0:
        return x
    return pltpu.roll(jnp.where(lane >= rows - j, halo, x), j, 1)


def near_kernel(taps, q_ref, k_ref, v_ref, cot_ref, halo_ref, w_ref, pow_ref, spec_ref,
                place_ref, dft_ref, inv_ref, mom_ref, back_ref, laghi_ref, laglo_ref, pick_ref,
                qs_ref, ks_ref, vs_ref, near_ref, grad_ref, state_ref, res_ref):
    rows = q_ref.shape[1]
    lane = lax.broadcasted_iota(jnp.int32, q_ref.shape, 1)
    halos = mm_tn(halo_ref[...], place_ref[...])
    w = w_ref[...]
    short = []
    for i, ref in enumerate((q_ref, k_ref, v_ref)):
        x = ref[...].astype(F32)
        halo = halos[:, i * rows : (i + 1) * rows]
        total = jnp.zeros(x.shape, F32)
        for j in range(taps):
            at = i * taps + j
            total = total + w[:, at : at + 1] * shifted(x, halo, lane, j)
        short.append(total.astype(BF16))
    qs_ref[...], ks_ref[...], vs_ref[...] = short
    gated = (short[1].astype(F32) * short[2].astype(F32)).astype(BF16)
    gmix = (cot_ref[...].astype(F32) * short[0].astype(F32)).astype(BF16)
    gated2 = jnp.concatenate([gated, gated], 1)
    gmix2 = jnp.concatenate([gmix, gmix], 1)
    z = mm(gated2, dft_ref[...])
    g = mm(gmix2, dft_ref[...])
    h = spec_ref[...]
    zr, zi = z[:, :rows], z[:, rows:]
    gr, gi = g[:, :rows], g[:, rows:]
    hr, hi = h[:, :rows], h[:, rows:]
    fwd = jnp.concatenate([zr * hr - zi * hi, zr * hi + zi * hr], 1).astype(BF16)
    bwd = jnp.concatenate([gr * hr + gi * hi, gi * hr - gr * hi], 1).astype(BF16)
    lag = jnp.concatenate([gr * zr + gi * zi, gi * zr - gr * zi], 1)
    near = mm(fwd, inv_ref[...])
    near_ref[...] = near[:, :rows] + near[:, rows:]
    grad = mm(bwd, inv_ref[...])
    grad_ref[...] = grad[:, :rows] + grad[:, rows:]
    powers = pow_ref[...]
    pick = pick_ref[...]
    state = powers * mm(gated2, back_ref[...])
    modes = pick.shape[0]

    def folded(x):
        high, low = parts(x, 2)
        return mm_nt(pick, high) + mm_nt(pick, low)

    state_ref[:modes, :] = folded(state)
    state_ref[modes:, :] = folded(powers * mm(gmix2, mom_ref[...]))
    high, low = parts(lag, 2)
    moments = mm(high, laghi_ref[...]) + mm(low, laghi_ref[...]) + mm(high, laglo_ref[...])
    res_ref[...] = folded(powers * moments)


def far_kernel(taps, me_ref, q_ref, k_ref, v_ref, cot_ref, halo_ref, qs_ref, ks_ref, vs_ref,
               near_ref, grad_ref, pow_ref, all_ref, state_ref, res_ref, dec_ref, amp_ref, skip_ref,
               place_ref, out_ref, back_ref, pick_ref, sums_ref,
               mixed_ref, gq_ref, gk_ref, gv_ref, head_ref, part_ref):
    rows = q_ref.shape[1]
    lane = lax.broadcasted_iota(jnp.int32, q_ref.shape, 1)
    me = me_ref[0]
    count = all_ref.shape[0]
    modes = dec_ref.shape[0]
    dec = dec_ref[...]
    root = jnp.sqrt(2.0 * dec)
    one = jnp.exp(-dec)
    chunk = jnp.exp(-dec * float(rows))
    zero = jnp.zeros(dec.shape, F32)

    def ahead(p, s):
        return jnp.where(p < me, s * chunk + all_ref[p, :modes, :].astype(F32), s)

    def behind(i, r):
        p = count - 1 - i
        return jnp.where(p > me, r * chunk + all_ref[p, modes:, :].astype(F32), r)

    s_in = lax.fori_loop(0, count, ahead, zero, unroll=8)
    r_in = lax.fori_loop(0, count, behind, zero, unroll=8)
    part_ref[:modes, :] = root * (res_ref[...] + one * s_in * state_ref[modes:, :])
    gain = amp_ref[...] * root * one
    powers = pow_ref[...]
    pick = pick_ref[...]

    def spread(x, table_ref):
        high, low = parts(powers * exact(mm_tn, x, pick, 2), 2)
        full = mm(high, table_ref[...]) + mm(low, table_ref[...])
        return full[:, :rows] + full[:, rows:]

    conv = (near_ref[...] + spread(gain * s_in, out_ref)).astype(BF16)
    gconv = (grad_ref[...] + spread(gain * r_in, back_ref)).astype(BF16)
    skip = skip_ref[...]
    qs, ks, vs = qs_ref[...].astype(F32), ks_ref[...].astype(F32), vs_ref[...].astype(F32)
    cot = cot_ref[...].astype(F32)
    gated = (ks * vs).astype(BF16).astype(F32)
    gmix = (cot * qs).astype(BF16).astype(F32)
    mix = conv.astype(F32) + skip * gated
    mixed_ref[...] = (qs * mix).astype(BF16)
    gq = (cot * mix).astype(BF16)
    ggated = gconv.astype(F32) + skip * gmix
    gk = (ggated * vs).astype(BF16)
    gv = (ggated * ks).astype(BF16)
    gq_ref[...], gk_ref[...], gv_ref[...] = gq, gk, gv
    first = (lax.broadcasted_iota(jnp.int32, (8, rows), 0) == lax.broadcasted_iota(jnp.int32, (8, rows), 1)).astype(BF16)
    head_ref[...] = jnp.concatenate([mm_nt(first, x) for x in (gq, gk, gv)], 0).astype(BF16)
    halos = mm_tn(halo_ref[...], place_ref[...])
    products = []
    for i, (ref, grads) in enumerate(((q_ref, gq), (k_ref, gk), (v_ref, gv))):
        x = ref[...].astype(F32)
        values = grads.astype(F32)
        halo = halos[:, i * rows : (i + 1) * rows]
        for j in range(taps):
            products.append((values * shifted(x, halo, lane, j)).astype(BF16))
    products.append((gmix * gated).astype(BF16))
    sums = mm(jnp.concatenate(products, 1), sums_ref[...])
    part_ref[modes:, :] = sums.T[:24, :]


def last_kernel(taps, gq_ref, gk_ref, gv_ref, halo_ref, w_ref, place_ref, oq_ref, ok_ref, ov_ref):
    rows = gq_ref.shape[1]
    lane = lax.broadcasted_iota(jnp.int32, gq_ref.shape, 1)
    halos = mm_tn(halo_ref[...], place_ref[...])
    w = w_ref[...]
    for i, (ref, out) in enumerate(((gq_ref, oq_ref), (gk_ref, ok_ref), (gv_ref, ov_ref))):
        x = ref[...].astype(F32)
        halo = halos[:, i * rows : (i + 1) * rows]
        total = jnp.zeros(x.shape, F32)
        for j in range(taps):
            moved = x if j == 0 else pltpu.roll(jnp.where(lane < j, halo, x), rows - j, 1)
            at = i * taps + j
            total = total + w[:, at : at + 1] * moved
        out[...] = total.astype(BF16)


def passed_along(block, axis, distance):
    devices = range(lax.axis_size(axis))
    route = [(i - distance, i) for i in devices if i - distance in devices]
    return lax.ppermute(block, axis, route)


def per_device(
    queries, key_signal, value_signal, cotangent, short_weight, residues, decay_rates, skip_gain
):
    channels, rows = queries.shape
    taps = short_weight.shape[1]
    modes = residues.shape[1]
    devices = lax.axis_size("ctx")
    block = min(256, channels)
    grid = (channels // block,)
    tab = {name: jnp.asarray(value) for name, value in tables(rows, modes).items()}
    wide = modes * NODES
    tail = np.zeros((24, 3 * rows), np.float32)
    head = np.zeros((24, 3 * rows), np.float32)
    for i in range(3):
        for j in range(8):
            tail[i * 8 + j, i * rows + rows - 8 + j] = 1
            head[i * 8 + j, i * rows + j] = 1
    tail, head = jnp.asarray(tail, BF16), jnp.asarray(head, BF16)
    sums = np.zeros(((3 * taps + 1) * rows, 128), np.float32)
    for i in range(3 * taps + 1):
        sums[i * rows : (i + 1) * rows, i] = 1
    sums = jnp.asarray(sums, BF16)

    def tall(width):
        return pl.BlockSpec((block, width), lambda i: (i, 0))

    def flat(height):
        return pl.BlockSpec((height, block), lambda i: (0, i))

    def whole(x):
        return pl.BlockSpec(x.shape, lambda i: (0,) * x.ndim)

    def shape(*dims, kind=F32):
        return jax.ShapeDtypeStruct(dims, kind)

    params = pltpu.CompilerParams(vmem_limit_bytes=48 * 1024 * 1024)
    sent = jnp.concatenate([x[:, rows - 8 :].T for x in (queries, key_signal, value_signal)], 0)
    left = passed_along(sent, "ctx", 1)
    w_tall = short_weight.reshape(3 * taps, channels).T
    dec_flat = decay_rates.T
    amp_flat = residues.T
    skip = skip_gain[:, None]

    args = (tab["times"], tab["pick"], tab["spec_hi"], tab["spec_lo"])
    powers, spec = pl.pallas_call(
        powers_kernel,
        grid=grid,
        in_specs=[tall(modes), tall(modes)] + [whole(x) for x in args],
        out_specs=[tall(wide), tall(2 * rows)],
        out_shape=[shape(channels, wide), shape(channels, 2 * rows)],
        compiler_params=params,
        cost_estimate=pl.CostEstimate(flops=10**9, bytes_accessed=5 * 10**6, transcendentals=10**6),
        name="powers",
    )(decay_rates, residues, *args)

    args = (tail, tab["dft"], tab["inv"], tab["mom"], tab["mom_back"], tab["lag_hi"], tab["lag_lo"], tab["pick"])
    q_short, k_short, v_short, near, grad, state, res = pl.pallas_call(
        functools.partial(near_kernel, taps),
        grid=grid,
        in_specs=[tall(rows)] * 4 + [flat(24), tall(3 * taps), tall(wide), tall(2 * rows)] + [whole(x) for x in args],
        out_specs=[tall(rows)] * 5 + [flat(2 * modes), flat(modes)],
        out_shape=[shape(channels, rows, kind=BF16)] * 3 + [shape(channels, rows)] * 2 + [shape(2 * modes, channels), shape(modes, channels)],
        compiler_params=params,
        name="near",
    )(queries, key_signal, value_signal, cotangent, left, w_tall, powers, spec, *args)

    every = lax.all_gather(state.astype(BF16), "ctx")
    me = lax.axis_index("ctx").astype(jnp.int32).reshape(1)
    args = (tail, tab["out"], tab["out_back"], tab["pick"], sums)
    mixed, gq, gk, gv, heads, part = pl.pallas_call(
        functools.partial(far_kernel, taps),
        grid=grid,
        in_specs=[pl.BlockSpec(memory_space=pltpu.SMEM)] + [tall(rows)] * 4 + [flat(24)] + [tall(rows)] * 5
        + [tall(wide), pl.BlockSpec((devices, 2 * modes, block), lambda i: (0, 0, i)), flat(2 * modes), flat(modes), flat(modes), flat(modes), tall(1)]
        + [whole(x) for x in args],
        out_specs=[tall(rows)] * 4 + [flat(24), flat(modes + 24)],
        out_shape=[shape(channels, rows, kind=BF16)] * 4 + [shape(24, channels, kind=BF16), shape(modes + 24, channels)],
        compiler_params=params,
        name="far",
    )(me, queries, key_signal, value_signal, cotangent, left, q_short, k_short, v_short, near, grad,
      powers, every, state, res, dec_flat, amp_flat, skip, *args)

    right = passed_along(heads, "ctx", -1)
    totals = lax.psum(part, "ctx") * (1.0 / math.sqrt(rows * devices))
    grads = pl.pallas_call(
        functools.partial(last_kernel, taps),
        grid=grid,
        in_specs=[tall(rows)] * 3 + [flat(24), tall(3 * taps), whole(head)],
        out_specs=[tall(rows)] * 3,
        out_shape=[shape(channels, rows, kind=BF16)] * 3,
        compiler_params=params,
        cost_estimate=pl.CostEstimate(flops=10**9, bytes_accessed=5 * 10**6, transcendentals=0),
        name="last",
    )(gq, gk, gv, right, w_tall, head)
    return (
        mixed,
        *grads,
        totals[modes : modes + 3 * taps].reshape(3, taps, channels),
        totals[:modes].T,
        totals[modes + 3 * taps],
    )


def solution(mesh):
    signal = P("tp", "ctx")
    in_specs = (signal,) * 4 + (P(None, None, "tp"), P("tp", None), P("tp", None), P("tp"))
    out_specs = (signal,) * 4 + (P(None, None, "tp"), P("tp", None), P("tp"))
    return jax.shard_map(
        per_device, mesh=mesh, in_specs=in_specs, out_specs=out_specs, check_vma=False
    )
```

```python
import functools
import math

import jax
import jax.numpy as jnp
import ml_dtypes
import numpy as np
from jax import lax
from jax.experimental import pallas as pl
from jax.experimental.pallas import tpu as pltpu
from jax.sharding import PartitionSpec as P

F32 = jnp.float32
BF16 = jnp.bfloat16
NODES = 16


def two(table):
    high = table.astype(ml_dtypes.bfloat16)
    low = (table - high.astype(np.float64)).astype(ml_dtypes.bfloat16)
    return high, low


@functools.lru_cache(None)
def tables(rows, modes):
    top = rows - 1
    half = [round(top / 2 - top / 2 * math.cos((2 * k + 1) * math.pi / (2 * NODES))) for k in range(NODES // 2)]
    nodes = np.array(half + [top - x for x in half[::-1]], np.float64)
    basis = np.ones((NODES, rows))
    spots = np.arange(rows, dtype=np.float64)
    for k in range(NODES):
        for other in range(NODES):
            if other != k:
                basis[k] *= (spots - nodes[other]) / (nodes[k] - nodes[other])
    spread = np.tile(basis, (modes, 1))
    back = spread[:, ::-1]
    omega = 2 * math.pi * (np.arange(rows) + 0.5) / (2 * rows)
    angle = spots[:, None] * omega[None, :]
    dft = np.concatenate([np.cos(angle), -np.sin(angle)], 1)
    inv = np.concatenate([np.cos(angle), -np.sin(angle)], 1).T / rows
    out = {}
    out["dft"] = np.concatenate(two(dft), 0)
    out["inv"] = np.concatenate(two(inv), 1)
    out["spec_hi"], out["spec_lo"] = two(spread @ dft)
    out["mom"] = np.concatenate(two(spread.T), 0)
    out["mom_back"] = np.concatenate(two(back.T), 0)
    out["lag_hi"], out["lag_lo"] = two(inv @ spread.T)
    out["out"] = np.concatenate(two(spread), 1)
    out["out_back"] = np.concatenate(two(back), 1)
    eye = np.eye(modes)
    out["times"] = np.kron(eye, nodes[None, :]).astype(ml_dtypes.bfloat16)
    pick = np.kron(eye, np.ones((1, NODES)))
    out["pick"] = pick.astype(ml_dtypes.bfloat16)
    return out


def mm(a, b):
    return lax.dot_general(a, b, (((1,), (0,)), ((), ())), preferred_element_type=F32)


def mm_nt(a, b):
    return lax.dot_general(a, b, (((1,), (1,)), ((), ())), preferred_element_type=F32)


def mm_tn(a, b):
    return lax.dot_general(a, b, (((0,), (0,)), ((), ())), preferred_element_type=F32)


def parts(x, count):
    out = []
    for _ in range(count):
        piece = x.astype(BF16)
        out.append(piece)
        x = x - piece.astype(F32)
    return out


def exact(op, x, table, count):
    total = None
    for piece in parts(x, count):
        term = op(piece, table)
        total = term if total is None else total + term
    return total


def powers_kernel(dec_ref, res_ref, times_ref, pick_ref, hi_ref, lo_ref, pow_ref, spec_ref):
    dec = dec_ref[...]
    gain = res_ref[...] * jnp.sqrt(2.0 * dec)
    powers = jnp.exp(-exact(mm, dec, times_ref[...], 3))
    pow_ref[...] = powers
    high, low = parts(powers * exact(mm, gain, pick_ref[...], 3), 2)
    spec_ref[...] = mm(high, hi_ref[...]) + mm(low, hi_ref[...]) + mm(high, lo_ref[...])


def shifted(x, halo, lane, j):
    rows = x.shape[1]
    if j == 0:
        return x
    return pltpu.roll(jnp.where(lane >= rows - j, halo, x), j, 1)


def near_kernel(taps, q_ref, k_ref, v_ref, cot_ref, halo_ref, w_ref, pow_ref, spec_ref,
                place_ref, dft_ref, inv_ref, mom_ref, back_ref, laghi_ref, laglo_ref, pick_ref,
                qs_ref, ks_ref, vs_ref, near_ref, grad_ref, state_ref, res_ref):
    rows = q_ref.shape[1]
    lane = lax.broadcasted_iota(jnp.int32, q_ref.shape, 1)
    halos = mm_tn(halo_ref[...], place_ref[...])
    w = w_ref[...]
    short = []
    for i, ref in enumerate((q_ref, k_ref, v_ref)):
        x = ref[...].astype(F32)
        halo = halos[:, i * rows : (i + 1) * rows]
        total = jnp.zeros(x.shape, F32)
        for j in range(taps):
            at = i * taps + j
            total = total + w[:, at : at + 1] * shifted(x, halo, lane, j)
        short.append(total.astype(BF16))
    qs_ref[...], ks_ref[...], vs_ref[...] = short
    gated = (short[1].astype(F32) * short[2].astype(F32)).astype(BF16)
    gmix = (cot_ref[...].astype(F32) * short[0].astype(F32)).astype(BF16)
    gated2 = jnp.concatenate([gated, gated], 1)
    gmix2 = jnp.concatenate([gmix, gmix], 1)
    z = mm(gated2, dft_ref[...])
    g = mm(gmix2, dft_ref[...])
    h = spec_ref[...]
    zr, zi = z[:, :rows], z[:, rows:]
    gr, gi = g[:, :rows], g[:, rows:]
    hr, hi = h[:, :rows], h[:, rows:]
    fwd = jnp.concatenate([zr * hr - zi * hi, zr * hi + zi * hr], 1).astype(BF16)
    bwd = jnp.concatenate([gr * hr + gi * hi, gi * hr - gr * hi], 1).astype(BF16)
    lag = jnp.concatenate([gr * zr + gi * zi, gi * zr - gr * zi], 1)
    near = mm(fwd, inv_ref[...])
    near_ref[...] = near[:, :rows] + near[:, rows:]
    grad = mm(bwd, inv_ref[...])
    grad_ref[...] = grad[:, :rows] + grad[:, rows:]
    powers = pow_ref[...]
    pick = pick_ref[...]
    state = powers * mm(gated2, back_ref[...])
    modes = pick.shape[0]

    def folded(x):
        high, low = parts(x, 2)
        return mm_nt(pick, high) + mm_nt(pick, low)

    state_ref[:modes, :] = folded(state)
    state_ref[modes:, :] = folded(powers * mm(gmix2, mom_ref[...]))
    high, low = parts(lag, 2)
    moments = mm(high, laghi_ref[...]) + mm(low, laghi_ref[...]) + mm(high, laglo_ref[...])
    res_ref[...] = folded(powers * moments)


def far_kernel(taps, q_ref, k_ref, v_ref, cot_ref, halo_ref, qs_ref, ks_ref, vs_ref,
               near_ref, grad_ref, pow_ref, all_ref, state_ref, res_ref, dec_ref, amp_ref, skip_ref,
               place_ref, out_ref, back_ref, pick_ref, sums_ref,
               mixed_ref, gq_ref, gk_ref, gv_ref, head_ref, part_ref):
    rows = q_ref.shape[1]
    lane = lax.broadcasted_iota(jnp.int32, q_ref.shape, 1)
    modes = dec_ref.shape[0]
    dec = dec_ref[...]
    root = jnp.sqrt(2.0 * dec)
    one = jnp.exp(-dec)
    s_in = all_ref[:modes, :]
    r_in = all_ref[modes:, :]
    part_ref[:modes, :] = root * (res_ref[...] + one * s_in * state_ref[modes:, :])
    gain = amp_ref[...] * root * one
    powers = pow_ref[...]
    pick = pick_ref[...]

    def spread(x, table_ref):
        high, low = parts(powers * exact(mm_tn, x, pick, 2), 2)
        full = mm(high, table_ref[...]) + mm(low, table_ref[...])
        return full[:, :rows] + full[:, rows:]

    conv = (near_ref[...] + spread(gain * s_in, out_ref)).astype(BF16)
    gconv = (grad_ref[...] + spread(gain * r_in, back_ref)).astype(BF16)
    skip = skip_ref[...]
    qs, ks, vs = qs_ref[...].astype(F32), ks_ref[...].astype(F32), vs_ref[...].astype(F32)
    cot = cot_ref[...].astype(F32)
    gated = (ks * vs).astype(BF16).astype(F32)
    gmix = (cot * qs).astype(BF16).astype(F32)
    mix = conv.astype(F32) + skip * gated
    mixed_ref[...] = (qs * mix).astype(BF16)
    gq = (cot * mix).astype(BF16)
    ggated = gconv.astype(F32) + skip * gmix
    gk = (ggated * vs).astype(BF16)
    gv = (ggated * ks).astype(BF16)
    gq_ref[...], gk_ref[...], gv_ref[...] = gq, gk, gv
    first = (lax.broadcasted_iota(jnp.int32, (8, rows), 0) == lax.broadcasted_iota(jnp.int32, (8, rows), 1)).astype(BF16)
    head_ref[...] = jnp.concatenate([mm_nt(first, x) for x in (gq, gk, gv)], 0).astype(BF16)
    halos = mm_tn(halo_ref[...], place_ref[...])
    products = []
    for i, (ref, grads) in enumerate(((q_ref, gq), (k_ref, gk), (v_ref, gv))):
        x = ref[...].astype(F32)
        values = grads.astype(F32)
        halo = halos[:, i * rows : (i + 1) * rows]
        for j in range(taps):
            products.append((values * shifted(x, halo, lane, j)).astype(BF16))
    products.append((gmix * gated).astype(BF16))
    sums = mm(jnp.concatenate(products, 1), sums_ref[...])
    part_ref[modes:, :] = sums.T[:32, :]


def last_kernel(taps, gq_ref, gk_ref, gv_ref, halo_ref, w_ref, place_ref, oq_ref, ok_ref, ov_ref):
    rows = gq_ref.shape[1]
    lane = lax.broadcasted_iota(jnp.int32, gq_ref.shape, 1)
    halos = mm_tn(halo_ref[...], place_ref[...])
    w = w_ref[...]
    for i, (ref, out) in enumerate(((gq_ref, oq_ref), (gk_ref, ok_ref), (gv_ref, ov_ref))):
        x = ref[...].astype(F32)
        halo = halos[:, i * rows : (i + 1) * rows]
        total = jnp.zeros(x.shape, F32)
        for j in range(taps):
            moved = x if j == 0 else pltpu.roll(jnp.where(lane < j, halo, x), rows - j, 1)
            at = i * taps + j
            total = total + w[:, at : at + 1] * moved
        out[...] = total.astype(BF16)


def partners(axis):
    n = lax.axis_size(axis)
    me = lax.axis_index(axis)
    barrier = pltpu.get_barrier_semaphore()
    where = [lax.rem(me + d, n) for d in range(n)]
    for d in range(1, n):
        pl.semaphore_signal(barrier, inc=1, device_id={axis: where[d]}, device_id_type=pl.DeviceIdType.MESH)
    pl.semaphore_wait(barrier, n - 1)
    return n, me, where


def send(src, dst, send_sem, recv_sem, axis, target):
    copy = pltpu.make_async_remote_copy(
        src_ref=src, dst_ref=dst, send_sem=send_sem, recv_sem=recv_sem,
        device_id={axis: target}, device_id_type=pl.DeviceIdType.MESH)
    copy.start()
    return copy


def gather_kernel(rows, state_ref, dec_ref, in_ref, out, got, send_sem, recv_sem):
    modes = dec_ref.shape[0]
    out[0] = state_ref[:modes, :].astype(BF16)
    out[1] = state_ref[modes:, :].astype(BF16)
    n, me, where = partners("ctx")
    copies = []
    for d in range(1, n):
        kind = jnp.where(where[d] > me, 0, 1)
        copies.append(send(out.at[kind], got.at[d], send_sem.at[d], recv_sem.at[d], "ctx", where[d]))
    chunk = jnp.exp(-dec_ref[...] * float(rows))
    for copy in copies:
        copy.wait()
    s = jnp.zeros(chunk.shape, F32)
    for d in range(n - 1, 0, -1):
        s = jnp.where(me >= d, s * chunk + got[d].astype(F32), s)
    in_ref[:modes, :] = s
    r = jnp.zeros(chunk.shape, F32)
    for d in range(1, n):
        r = jnp.where(me < d, r * chunk + got[d].astype(F32), r)
    in_ref[modes:, :] = r


def reduce_kernel(scale, part_ref, head_ref, total_ref, halo_ref, parted, got, mine, full, heads,
                  send_sem, recv_sem, back_send, back_recv, halo_sem):
    n = lax.axis_size("ctx")
    width = parted.shape[2]
    for p in range(n):
        parted[p] = part_ref[:, p * width : (p + 1) * width].astype(BF16)
    n, me, where = partners("ctx")
    halo = send(head_ref, heads, halo_sem.at[0], halo_sem.at[1], "ctx", where[n - 1])
    copies = []
    for d in range(1, n):
        copies.append(send(parted.at[where[d]], got.at[d], send_sem.at[d], recv_sem.at[d], "ctx", where[d]))
    total = parted[me].astype(F32)
    for d in range(1, n):
        copies[d - 1].wait()
        total = total + got[d].astype(F32)
    mine[...] = (total * scale).astype(BF16)
    copies = []
    for d in range(1, n):
        copies.append(send(mine, full.at[d], back_send.at[d], back_recv.at[d], "ctx", where[d]))
    full[0] = mine[...]
    halo.wait()
    halo_ref[...] = jnp.where(me < n - 1, heads[...].astype(F32), 0.0).astype(BF16)
    for copy in copies:
        copy.wait()
    for p in range(n):
        total_ref[:, p * width : (p + 1) * width] = full[lax.rem(me - p + n, n)].astype(F32)


def passed_along(block, axis, distance):
    devices = range(lax.axis_size(axis))
    route = [(i - distance, i) for i in devices if i - distance in devices]
    return lax.ppermute(block, axis, route)


def per_device(
    queries, key_signal, value_signal, cotangent, short_weight, residues, decay_rates, skip_gain
):
    channels, rows = queries.shape
    taps = short_weight.shape[1]
    modes = residues.shape[1]
    devices = lax.axis_size("ctx")
    block = min(256, channels)
    grid = (channels // block,)
    tab = {name: jnp.asarray(value) for name, value in tables(rows, modes).items()}
    wide = modes * NODES
    tail = np.zeros((24, 3 * rows), np.float32)
    head = np.zeros((24, 3 * rows), np.float32)
    for i in range(3):
        for j in range(8):
            tail[i * 8 + j, i * rows + rows - 8 + j] = 1
            head[i * 8 + j, i * rows + j] = 1
    tail, head = jnp.asarray(tail, BF16), jnp.asarray(head, BF16)
    sums = np.zeros(((3 * taps + 1) * rows, 128), np.float32)
    for i in range(3 * taps + 1):
        sums[i * rows : (i + 1) * rows, i] = 1
    sums = jnp.asarray(sums, BF16)

    def tall(width):
        return pl.BlockSpec((block, width), lambda i: (i, 0))

    def flat(height):
        return pl.BlockSpec((height, block), lambda i: (0, i))

    def whole(x):
        return pl.BlockSpec(x.shape, lambda i: (0,) * x.ndim)

    def shape(*dims, kind=F32):
        return jax.ShapeDtypeStruct(dims, kind)

    params = pltpu.CompilerParams(vmem_limit_bytes=60 * 1024 * 1024)
    sent = jnp.concatenate([x[:, rows - 8 :].T for x in (queries, key_signal, value_signal)], 0)
    left = passed_along(sent, "ctx", 1)
    w_tall = short_weight.reshape(3 * taps, channels).T
    dec_flat = decay_rates.T
    amp_flat = residues.T
    skip = skip_gain[:, None]

    args = (tab["times"], tab["pick"], tab["spec_hi"], tab["spec_lo"])
    powers, spec = pl.pallas_call(
        powers_kernel,
        grid=grid,
        in_specs=[tall(modes), tall(modes)] + [whole(x) for x in args],
        out_specs=[tall(wide), tall(2 * rows)],
        out_shape=[shape(channels, wide), shape(channels, 2 * rows)],
        compiler_params=params,
        cost_estimate=pl.CostEstimate(flops=10**9, bytes_accessed=5 * 10**6, transcendentals=10**6),
        name="powers",
    )(decay_rates, residues, *args)

    args = (tail, tab["dft"], tab["inv"], tab["mom"], tab["mom_back"], tab["lag_hi"], tab["lag_lo"], tab["pick"])
    q_short, k_short, v_short, near, grad, state, res = pl.pallas_call(
        functools.partial(near_kernel, taps),
        grid=grid,
        in_specs=[tall(rows)] * 4 + [flat(24), tall(3 * taps), tall(wide), tall(2 * rows)] + [whole(x) for x in args],
        out_specs=[tall(rows)] * 5 + [flat(2 * modes), flat(modes)],
        out_shape=[shape(channels, rows, kind=BF16)] * 3 + [shape(channels, rows)] * 2 + [shape(2 * modes, channels), shape(modes, channels)],
        compiler_params=params,
        name="near",
    )(queries, key_signal, value_signal, cotangent, left, w_tall, powers, spec, *args)

    dma = pltpu.SemaphoreType.DMA
    vmem = pl.BlockSpec(memory_space=pltpu.VMEM)
    every = pl.pallas_call(
        functools.partial(gather_kernel, rows),
        in_specs=[vmem] * 2,
        out_specs=vmem,
        out_shape=shape(2 * modes, channels),
        scratch_shapes=[
            pltpu.VMEM((2, modes, channels), BF16), pltpu.VMEM((devices, modes, channels), BF16),
            dma((devices,)), dma((devices,)),
        ],
        compiler_params=pltpu.CompilerParams(collective_id=0, has_side_effects=True, vmem_limit_bytes=32 * 1024 * 1024),
        name="gather",
    )(state, dec_flat)
    args = (tail, tab["out"], tab["out_back"], tab["pick"], sums)
    mixed, gq, gk, gv, heads, part = pl.pallas_call(
        functools.partial(far_kernel, taps),
        grid=grid,
        in_specs=[tall(rows)] * 4 + [flat(24)] + [tall(rows)] * 5
        + [tall(wide), flat(2 * modes), flat(2 * modes), flat(modes), flat(modes), flat(modes), tall(1)]
        + [whole(x) for x in args],
        out_specs=[tall(rows)] * 4 + [flat(24), flat(modes + 32)],
        out_shape=[shape(channels, rows, kind=BF16)] * 4 + [shape(24, channels, kind=BF16), shape(modes + 32, channels)],
        compiler_params=params,
        name="far",
    )(queries, key_signal, value_signal, cotangent, left, q_short, k_short, v_short, near, grad,
      powers, every, state, res, dec_flat, amp_flat, skip, *args)

    scale = 1.0 / math.sqrt(rows * devices)
    width = channels // devices
    if width % 128 == 0:
        height = modes + 32
        totals, right = pl.pallas_call(
            functools.partial(reduce_kernel, scale),
            in_specs=[vmem] * 2,
            out_specs=[vmem] * 2,
            out_shape=[shape(height, channels), shape(24, channels, kind=BF16)],
            scratch_shapes=[
                pltpu.VMEM((devices, height, width), BF16), pltpu.VMEM((devices, height, width), BF16),
                pltpu.VMEM((height, width), BF16), pltpu.VMEM((devices, height, width), BF16),
                pltpu.VMEM((24, channels), BF16),
                dma((devices,)), dma((devices,)), dma((devices,)), dma((devices,)), dma((2,)),
            ],
            compiler_params=pltpu.CompilerParams(collective_id=1, has_side_effects=True, vmem_limit_bytes=32 * 1024 * 1024),
            name="reduce",
        )(part, heads)
    else:
        right = passed_along(heads, "ctx", -1)
        totals = lax.psum(part, "ctx") * scale
    grads = pl.pallas_call(
        functools.partial(last_kernel, taps),
        grid=grid,
        in_specs=[tall(rows)] * 3 + [flat(24), tall(3 * taps), whole(head)],
        out_specs=[tall(rows)] * 3,
        out_shape=[shape(channels, rows, kind=BF16)] * 3,
        compiler_params=params,
        cost_estimate=pl.CostEstimate(flops=10**9, bytes_accessed=5 * 10**6, transcendentals=0),
        name="last",
    )(gq, gk, gv, right, w_tall, head)
    return (
        mixed,
        *grads,
        totals[modes : modes + 3 * taps].reshape(3, taps, channels),
        totals[:modes].T,
        totals[modes + 3 * taps],
    )


def solution(mesh):
    signal = P("tp", "ctx")
    in_specs = (signal,) * 4 + (P(None, None, "tp"), P("tp", None), P("tp", None), P("tp"))
    out_specs = (signal,) * 4 + (P(None, None, "tp"), P("tp", None), P("tp"))
    return jax.shard_map(
        per_device, mesh=mesh, in_specs=in_specs, out_specs=out_specs, check_vma=False
    )
```

```python
import functools
import math

import jax
import jax.numpy as jnp
import ml_dtypes
import numpy as np
from jax import lax
from jax.experimental import pallas as pl
from jax.experimental.pallas import tpu as pltpu
from jax.sharding import PartitionSpec as P

F32 = jnp.float32
BF16 = jnp.bfloat16
NODES = 16


def two(table):
    high = table.astype(ml_dtypes.bfloat16)
    low = (table - high.astype(np.float64)).astype(ml_dtypes.bfloat16)
    return high, low


@functools.lru_cache(None)
def tables(rows, modes):
    top = rows - 1
    half = [round(top / 2 - top / 2 * math.cos((2 * k + 1) * math.pi / (2 * NODES))) for k in range(NODES // 2)]
    nodes = np.array(half + [top - x for x in half[::-1]], np.float64)
    basis = np.ones((NODES, rows))
    spots = np.arange(rows, dtype=np.float64)
    for k in range(NODES):
        for other in range(NODES):
            if other != k:
                basis[k] *= (spots - nodes[other]) / (nodes[k] - nodes[other])
    spread = np.tile(basis, (modes, 1))
    back = spread[:, ::-1]
    omega = 2 * math.pi * (np.arange(rows) + 0.5) / (2 * rows)
    angle = spots[:, None] * omega[None, :]
    dft = np.concatenate([np.cos(angle), -np.sin(angle)], 1)
    inv = np.concatenate([np.cos(angle), -np.sin(angle)], 1).T / rows
    out = {}
    out["dft"] = np.concatenate(two(dft), 0)
    out["inv"] = np.concatenate(two(inv), 1)
    out["spec_hi"], out["spec_lo"] = two(spread @ dft)
    out["mom"] = np.concatenate(two(spread.T), 0)
    out["mom_back"] = np.concatenate(two(back.T), 0)
    out["lag_hi"], out["lag_lo"] = two(inv @ spread.T)
    out["out"] = np.concatenate(two(spread), 1)
    out["out_back"] = np.concatenate(two(back), 1)
    eye = np.eye(modes)
    out["times"] = np.kron(eye, nodes[None, :]).astype(ml_dtypes.bfloat16)
    pick = np.kron(eye, np.ones((1, NODES)))
    out["pick"] = pick.astype(ml_dtypes.bfloat16)
    return out


def mm(a, b):
    return lax.dot_general(a, b, (((1,), (0,)), ((), ())), preferred_element_type=F32)


def mm_nt(a, b):
    return lax.dot_general(a, b, (((1,), (1,)), ((), ())), preferred_element_type=F32)


def mm_tn(a, b):
    return lax.dot_general(a, b, (((0,), (0,)), ((), ())), preferred_element_type=F32)


def parts(x, count):
    out = []
    for _ in range(count):
        piece = x.astype(BF16)
        out.append(piece)
        x = x - piece.astype(F32)
    return out


def exact(op, x, table, count):
    total = None
    for piece in parts(x, count):
        term = op(piece, table)
        total = term if total is None else total + term
    return total


def powers_kernel(dec_ref, res_ref, times_ref, pick_ref, hi_ref, lo_ref, eye_ref, pow_ref, spec_ref, flat_ref):
    dec = dec_ref[...]
    modes = dec.shape[1]
    flat_ref[:modes, :] = exact(lambda x, eye: mm_nt(eye, x), dec, eye_ref[...], 3)
    flat_ref[modes:, :] = exact(lambda x, eye: mm_nt(eye, x), res_ref[...], eye_ref[...], 3)
    gain = res_ref[...] * jnp.sqrt(2.0 * dec)
    powers = jnp.exp(-exact(mm, dec, times_ref[...], 3))
    pow_ref[...] = powers
    high, low = parts(powers * exact(mm, gain, pick_ref[...], 3), 2)
    spec_ref[...] = mm(high, hi_ref[...]) + mm(low, hi_ref[...]) + mm(high, lo_ref[...])


def moved(x, halo, table):
    return mm(jnp.concatenate([x, halo.astype(BF16)], 1), table)


def weights_wide(w_ref, wide_ref):
    return mm_tn(jnp.concatenate(parts(w_ref[...], 3), 0), wide_ref[...])


def tap_sum(shifts, w, i, taps, rows):
    total = None
    for j in range(taps):
        at = (i * taps + j) * rows
        term = w[:, at : at + rows] * shifts[:, j * rows : (j + 1) * rows]
        total = term if total is None else total + term
    return total


def near_kernel(taps, q_ref, k_ref, v_ref, cot_ref, halo_ref, w_ref, pow_ref, spec_ref,
                place_ref, shift_ref, wide_ref, dft_ref, inv_ref, mom_ref, back_ref, laghi_ref, laglo_ref, pick_ref,
                qs_ref, ks_ref, vs_ref, near_ref, grad_ref, state_ref, res_ref):
    rows = q_ref.shape[1]
    halos = mm_tn(halo_ref[...], place_ref[...])
    w = weights_wide(w_ref, wide_ref)
    short = []
    for i, ref in enumerate((q_ref, k_ref, v_ref)):
        shifts = moved(ref[...], halos[:, i * rows : (i + 1) * rows], shift_ref[...])
        short.append(tap_sum(shifts, w, i, taps, rows).astype(BF16))
    qs_ref[...], ks_ref[...], vs_ref[...] = short
    gated = (short[1].astype(F32) * short[2].astype(F32)).astype(BF16)
    gmix = (cot_ref[...].astype(F32) * short[0].astype(F32)).astype(BF16)
    gated2 = jnp.concatenate([gated, gated], 1)
    gmix2 = jnp.concatenate([gmix, gmix], 1)
    z = mm(gated2, dft_ref[...])
    g = mm(gmix2, dft_ref[...])
    h = spec_ref[...]
    zr, zi = z[:, :rows], z[:, rows:]
    gr, gi = g[:, :rows], g[:, rows:]
    hr, hi = h[:, :rows], h[:, rows:]
    fwd = jnp.concatenate([zr * hr - zi * hi, zr * hi + zi * hr], 1).astype(BF16)
    bwd = jnp.concatenate([gr * hr + gi * hi, gi * hr - gr * hi], 1).astype(BF16)
    lag = jnp.concatenate([gr * zr + gi * zi, gi * zr - gr * zi], 1)
    near = mm(fwd, inv_ref[...])
    near_ref[...] = near[:, :rows] + near[:, rows:]
    grad = mm(bwd, inv_ref[...])
    grad_ref[...] = grad[:, :rows] + grad[:, rows:]
    powers = pow_ref[...]
    pick = pick_ref[...]
    state = powers * mm(gated2, back_ref[...])
    modes = pick.shape[0]

    def folded(x):
        high, low = parts(x, 2)
        return mm_nt(pick, high) + mm_nt(pick, low)

    state_ref[:modes, :] = folded(state)
    state_ref[modes:, :] = folded(powers * mm(gmix2, mom_ref[...]))
    high, low = parts(lag, 2)
    moments = mm(high, laghi_ref[...]) + mm(low, laghi_ref[...]) + mm(high, laglo_ref[...])
    res_ref[...] = folded(powers * moments)


def far_kernel(taps, q_ref, k_ref, v_ref, cot_ref, halo_ref, qs_ref, ks_ref, vs_ref,
               near_ref, grad_ref, pow_ref, all_ref, state_ref, res_ref, dec_ref, amp_ref, skip_ref,
               place_ref, shift_ref, ones_ref, out_ref, back_ref, pick_ref, sums_ref,
               mixed_ref, gq_ref, gk_ref, gv_ref, head_ref, part_ref):
    rows = q_ref.shape[1]
    modes = dec_ref.shape[0]
    dec = dec_ref[...]
    root = jnp.sqrt(2.0 * dec)
    one = jnp.exp(-dec)
    s_in = all_ref[:modes, :]
    r_in = all_ref[modes:, :]
    part_ref[:modes, :] = root * (res_ref[...] + one * s_in * state_ref[modes:, :])
    gain = amp_ref[...] * root * one
    powers = pow_ref[...]
    pick = pick_ref[...]

    def spread(x, table_ref):
        high, low = parts(powers * exact(mm_tn, x, pick, 2), 2)
        full = mm(high, table_ref[...]) + mm(low, table_ref[...])
        return full[:, :rows] + full[:, rows:]

    conv = (near_ref[...] + spread(gain * s_in, out_ref)).astype(BF16)
    gconv = (grad_ref[...] + spread(gain * r_in, back_ref)).astype(BF16)
    skip = exact(mm_tn, skip_ref[...], ones_ref[...], 3)
    qs, ks, vs = qs_ref[...].astype(F32), ks_ref[...].astype(F32), vs_ref[...].astype(F32)
    cot = cot_ref[...].astype(F32)
    gated = (ks * vs).astype(BF16).astype(F32)
    gmix = (cot * qs).astype(BF16).astype(F32)
    mix = conv.astype(F32) + skip * gated
    mixed_ref[...] = (qs * mix).astype(BF16)
    gq = (cot * mix).astype(BF16)
    ggated = gconv.astype(F32) + skip * gmix
    gk = (ggated * vs).astype(BF16)
    gv = (ggated * ks).astype(BF16)
    gq_ref[...], gk_ref[...], gv_ref[...] = gq, gk, gv
    first = (lax.broadcasted_iota(jnp.int32, (8, rows), 0) == lax.broadcasted_iota(jnp.int32, (8, rows), 1)).astype(BF16)
    head_ref[...] = jnp.concatenate([mm_nt(first, x) for x in (gq, gk, gv)], 0).astype(BF16)
    halos = mm_tn(halo_ref[...], place_ref[...])
    products = []
    for i, (ref, grads) in enumerate(((q_ref, gq), (k_ref, gk), (v_ref, gv))):
        values = grads.astype(F32)
        shifts = moved(ref[...], halos[:, i * rows : (i + 1) * rows], shift_ref[...])
        for j in range(taps):
            products.append((values * shifts[:, j * rows : (j + 1) * rows]).astype(BF16))
    products.append((gmix * gated).astype(BF16))
    sums = mm(jnp.concatenate(products, 1), sums_ref[...])
    part_ref[modes:, :] = sums.T[:32, :]


def last_kernel(taps, gq_ref, gk_ref, gv_ref, halo_ref, w_ref, place_ref, shift_ref, wide_ref, oq_ref, ok_ref, ov_ref):
    rows = gq_ref.shape[1]
    halos = mm_tn(halo_ref[...], place_ref[...])
    w = weights_wide(w_ref, wide_ref)
    for i, (ref, out) in enumerate(((gq_ref, oq_ref), (gk_ref, ok_ref), (gv_ref, ov_ref))):
        shifts = moved(ref[...], halos[:, i * rows : (i + 1) * rows], shift_ref[...])
        out[...] = tap_sum(shifts, w, i, taps, rows).astype(BF16)


def partners(axis):
    n = lax.axis_size(axis)
    me = lax.axis_index(axis)
    barrier = pltpu.get_barrier_semaphore()
    where = [lax.rem(me + d, n) for d in range(n)]
    for d in range(1, n):
        pl.semaphore_signal(barrier, inc=1, device_id={axis: where[d]}, device_id_type=pl.DeviceIdType.MESH)
    pl.semaphore_wait(barrier, n - 1)
    return n, me, where


def send(src, dst, send_sem, recv_sem, axis, target):
    copy = pltpu.make_async_remote_copy(
        src_ref=src, dst_ref=dst, send_sem=send_sem, recv_sem=recv_sem,
        device_id={axis: target}, device_id_type=pl.DeviceIdType.MESH)
    copy.start()
    return copy


def halo_kernel(q_ref, k_ref, v_ref, halo_ref, tails, got, sems):
    rows = q_ref.shape[1]
    shape = (8, rows)
    last = (lax.broadcasted_iota(jnp.int32, shape, 0) + (rows - 8) == lax.broadcasted_iota(jnp.int32, shape, 1)).astype(BF16)
    tails[...] = jnp.concatenate([mm_nt(last, ref[...]) for ref in (q_ref, k_ref, v_ref)], 0).astype(BF16)
    n = lax.axis_size("ctx")
    me = lax.axis_index("ctx")
    right, left = lax.rem(me + 1, n), lax.rem(me + n - 1, n)
    barrier = pltpu.get_barrier_semaphore()
    for other in (right, left):
        pl.semaphore_signal(barrier, inc=1, device_id={"ctx": other}, device_id_type=pl.DeviceIdType.MESH)
    pl.semaphore_wait(barrier, 2)
    send(tails, got, sems.at[0], sems.at[1], "ctx", right).wait()
    halo_ref[...] = jnp.where(me > 0, got[...].astype(F32), 0.0).astype(BF16)


def gather_kernel(rows, state_ref, dec_ref, in_ref, out, got, send_sem, recv_sem):
    modes = dec_ref.shape[0] // 2
    out[0] = state_ref[:modes, :].astype(BF16)
    out[1] = state_ref[modes:, :].astype(BF16)
    n, me, where = partners("ctx")
    copies = []
    for d in range(1, n):
        kind = jnp.where(where[d] > me, 0, 1)
        copies.append(send(out.at[kind], got.at[d], send_sem.at[d], recv_sem.at[d], "ctx", where[d]))
    chunk = jnp.exp(-dec_ref[:modes, :] * float(rows))
    for copy in copies:
        copy.wait()
    s = jnp.zeros(chunk.shape, F32)
    for d in range(n - 1, 0, -1):
        s = jnp.where(me >= d, s * chunk + got[d].astype(F32), s)
    in_ref[:modes, :] = s
    r = jnp.zeros(chunk.shape, F32)
    for d in range(1, n):
        r = jnp.where(me < d, r * chunk + got[d].astype(F32), r)
    in_ref[modes:, :] = r


def reduce_kernel(scale, part_ref, head_ref, total_ref, halo_ref, parted, got, mine, full, heads,
                  send_sem, recv_sem, back_send, back_recv, halo_sem):
    n = lax.axis_size("ctx")
    width = parted.shape[2]
    for p in range(n):
        parted[p] = part_ref[:, p * width : (p + 1) * width].astype(BF16)
    n, me, where = partners("ctx")
    halo = send(head_ref, heads, halo_sem.at[0], halo_sem.at[1], "ctx", where[n - 1])
    copies = []
    for d in range(1, n):
        copies.append(send(parted.at[where[d]], got.at[d], send_sem.at[d], recv_sem.at[d], "ctx", where[d]))
    total = parted[me].astype(F32)
    for d in range(1, n):
        copies[d - 1].wait()
        total = total + got[d].astype(F32)
    mine[...] = (total * scale).astype(BF16)
    copies = []
    for d in range(1, n):
        copies.append(send(mine, full.at[d], back_send.at[d], back_recv.at[d], "ctx", where[d]))
    full[0] = mine[...]
    halo.wait()
    halo_ref[...] = jnp.where(me < n - 1, heads[...].astype(F32), 0.0).astype(BF16)
    for copy in copies:
        copy.wait()
    for p in range(n):
        total_ref[:, p * width : (p + 1) * width] = full[lax.rem(me - p + n, n)].astype(F32)


def passed_along(block, axis, distance):
    devices = range(lax.axis_size(axis))
    route = [(i - distance, i) for i in devices if i - distance in devices]
    return lax.ppermute(block, axis, route)


def per_device(
    queries, key_signal, value_signal, cotangent, short_weight, residues, decay_rates, skip_gain
):
    channels, rows = queries.shape
    taps = short_weight.shape[1]
    modes = residues.shape[1]
    devices = lax.axis_size("ctx")
    block = min(256, channels)
    grid = (channels // block,)
    tab = {name: jnp.asarray(value) for name, value in tables(rows, modes).items()}
    wide = modes * NODES
    tail = np.zeros((24, 3 * rows), np.float32)
    head = np.zeros((24, 3 * rows), np.float32)
    for i in range(3):
        for j in range(8):
            tail[i * 8 + j, i * rows + rows - 8 + j] = 1
            head[i * 8 + j, i * rows + j] = 1
    tail, head = jnp.asarray(tail, BF16), jnp.asarray(head, BF16)
    sums = np.zeros(((3 * taps + 1) * rows, 128), np.float32)
    for i in range(3 * taps + 1):
        sums[i * rows : (i + 1) * rows, i] = 1
    sums = jnp.asarray(sums, BF16)

    def tall(width):
        return pl.BlockSpec((block, width), lambda i: (i, 0))

    def flat(height):
        return pl.BlockSpec((height, block), lambda i: (0, i))

    def whole(x):
        return pl.BlockSpec(x.shape, lambda i: (0,) * x.ndim)

    def shape(*dims, kind=F32):
        return jax.ShapeDtypeStruct(dims, kind)

    params = pltpu.CompilerParams(vmem_limit_bytes=60 * 1024 * 1024)
    dma = pltpu.SemaphoreType.DMA
    vmem = pl.BlockSpec(memory_space=pltpu.VMEM)
    left = pl.pallas_call(
        halo_kernel,
        in_specs=[vmem] * 3,
        out_specs=vmem,
        out_shape=shape(24, channels, kind=BF16),
        scratch_shapes=[pltpu.VMEM((24, channels), BF16)] * 2 + [dma((2,))],
        compiler_params=pltpu.CompilerParams(collective_id=2, has_side_effects=True, vmem_limit_bytes=60 * 1024 * 1024),
        name="halo",
    )(queries, key_signal, value_signal)
    w_flat = jnp.concatenate([short_weight.reshape(3 * taps, channels), jnp.zeros((24 - 3 * taps, channels), F32)], 0)
    skip = skip_gain[None, :]
    both = [np.zeros((2 * rows, taps * rows), np.float32) for _ in range(2)]
    for j in range(taps):
        for t in range(rows):
            both[0][t - j if t >= j else 2 * rows + t - j, j * rows + t] = 1
            both[1][t + j, j * rows + t] = 1
    before, after = (jnp.asarray(x, BF16) for x in both)
    spread_w = np.zeros((24, 3 * taps * rows), np.float32)
    for i in range(3 * taps):
        spread_w[i, i * rows : (i + 1) * rows] = 1
    spread_w = jnp.asarray(np.tile(spread_w, (3, 1)), BF16)

    args = (tab["times"], tab["pick"], tab["spec_hi"], tab["spec_lo"], jnp.eye(modes, dtype=BF16))
    powers, spec, flats = pl.pallas_call(
        powers_kernel,
        grid=grid,
        in_specs=[tall(modes), tall(modes)] + [whole(x) for x in args],
        out_specs=[tall(wide), tall(2 * rows), flat(2 * modes)],
        out_shape=[shape(channels, wide), shape(channels, 2 * rows), shape(2 * modes, channels)],
        compiler_params=params,
        cost_estimate=pl.CostEstimate(flops=10**9, bytes_accessed=5 * 10**6, transcendentals=10**6),
        name="powers",
    )(decay_rates, residues, *args)

    args = (tail, before, spread_w, tab["dft"], tab["inv"], tab["mom"], tab["mom_back"], tab["lag_hi"], tab["lag_lo"], tab["pick"])
    q_short, k_short, v_short, near, grad, state, res = pl.pallas_call(
        functools.partial(near_kernel, taps),
        grid=grid,
        in_specs=[tall(rows)] * 4 + [flat(24), flat(24), tall(wide), tall(2 * rows)] + [whole(x) for x in args],
        out_specs=[tall(rows)] * 5 + [flat(2 * modes), flat(modes)],
        out_shape=[shape(channels, rows, kind=BF16)] * 3 + [shape(channels, rows)] * 2 + [shape(2 * modes, channels), shape(modes, channels)],
        compiler_params=params,
        name="near",
    )(queries, key_signal, value_signal, cotangent, left, w_flat, powers, spec, *args)

    every = pl.pallas_call(
        functools.partial(gather_kernel, rows),
        in_specs=[vmem] * 2,
        out_specs=vmem,
        out_shape=shape(2 * modes, channels),
        scratch_shapes=[
            pltpu.VMEM((2, modes, channels), BF16), pltpu.VMEM((devices, modes, channels), BF16),
            dma((devices,)), dma((devices,)),
        ],
        compiler_params=pltpu.CompilerParams(collective_id=0, has_side_effects=True, vmem_limit_bytes=60 * 1024 * 1024),
        name="gather",
    )(state, flats)
    args = (tail, before, jnp.ones((1, rows), BF16), tab["out"], tab["out_back"], tab["pick"], sums)
    mixed, gq, gk, gv, heads, part = pl.pallas_call(
        functools.partial(far_kernel, taps),
        grid=grid,
        in_specs=[tall(rows)] * 4 + [flat(24)] + [tall(rows)] * 5
        + [tall(wide), flat(2 * modes), flat(2 * modes), flat(modes), flat(modes), pl.BlockSpec((modes, block), lambda i: (1, i)), flat(1)]
        + [whole(x) for x in args],
        out_specs=[tall(rows)] * 4 + [flat(24), flat(modes + 32)],
        out_shape=[shape(channels, rows, kind=BF16)] * 4 + [shape(24, channels, kind=BF16), shape(modes + 32, channels)],
        compiler_params=params,
        name="far",
    )(queries, key_signal, value_signal, cotangent, left, q_short, k_short, v_short, near, grad,
      powers, every, state, res, flats, flats, skip, *args)

    scale = 1.0 / math.sqrt(rows * devices)
    width = channels // devices
    if width % 128 == 0:
        height = modes + 32
        totals, right = pl.pallas_call(
            functools.partial(reduce_kernel, scale),
            in_specs=[vmem] * 2,
            out_specs=[vmem] * 2,
            out_shape=[shape(height, channels), shape(24, channels, kind=BF16)],
            scratch_shapes=[
                pltpu.VMEM((devices, height, width), BF16), pltpu.VMEM((devices, height, width), BF16),
                pltpu.VMEM((height, width), BF16), pltpu.VMEM((devices, height, width), BF16),
                pltpu.VMEM((24, channels), BF16),
                dma((devices,)), dma((devices,)), dma((devices,)), dma((devices,)), dma((2,)),
            ],
            compiler_params=pltpu.CompilerParams(collective_id=1, has_side_effects=True, vmem_limit_bytes=60 * 1024 * 1024),
            name="reduce",
        )(part, heads)
    else:
        right = passed_along(heads, "ctx", -1)
        totals = lax.psum(part, "ctx") * scale
    grads = pl.pallas_call(
        functools.partial(last_kernel, taps),
        grid=grid,
        in_specs=[tall(rows)] * 3 + [flat(24), flat(24), whole(head), whole(after), whole(spread_w)],
        out_specs=[tall(rows)] * 3,
        out_shape=[shape(channels, rows, kind=BF16)] * 3,
        compiler_params=params,
        cost_estimate=pl.CostEstimate(flops=10**9, bytes_accessed=5 * 10**6, transcendentals=0),
        name="last",
    )(gq, gk, gv, right, w_flat, head, after, spread_w)
    return (
        mixed,
        *grads,
        totals[modes : modes + 3 * taps].reshape(3, taps, channels),
        totals[:modes].T,
        totals[modes + 3 * taps],
    )


def solution(mesh):
    signal = P("tp", "ctx")
    in_specs = (signal,) * 4 + (P(None, None, "tp"), P("tp", None), P("tp", None), P("tp"))
    out_specs = (signal,) * 4 + (P(None, None, "tp"), P("tp", None), P("tp"))
    return jax.shard_map(
        per_device, mesh=mesh, in_specs=in_specs, out_specs=out_specs, check_vma=False
    )
```

```python
import functools
import math

import jax
import jax.numpy as jnp
import ml_dtypes
import numpy as np
from jax import lax
from jax.experimental import pallas as pl
from jax.experimental.pallas import tpu as pltpu
from jax.sharding import PartitionSpec as P

F32 = jnp.float32
BF16 = jnp.bfloat16
NODES = 16


def two(table):
    high = table.astype(ml_dtypes.bfloat16)
    low = (table - high.astype(np.float64)).astype(ml_dtypes.bfloat16)
    return high, low


@functools.lru_cache(None)
def tables(rows, modes):
    top = rows - 1
    half = [round(top / 2 - top / 2 * math.cos((2 * k + 1) * math.pi / (2 * NODES))) for k in range(NODES // 2)]
    nodes = np.array(half + [top - x for x in half[::-1]], np.float64)
    basis = np.ones((NODES, rows))
    spots = np.arange(rows, dtype=np.float64)
    for k in range(NODES):
        for other in range(NODES):
            if other != k:
                basis[k] *= (spots - nodes[other]) / (nodes[k] - nodes[other])
    spread = np.tile(basis, (modes, 1))
    back = spread[:, ::-1]
    omega = 2 * math.pi * (np.arange(rows) + 0.5) / (2 * rows)
    angle = spots[:, None] * omega[None, :]
    dft = np.concatenate([np.cos(angle), -np.sin(angle)], 1)
    inv = np.concatenate([np.cos(angle), -np.sin(angle)], 1).T / rows
    out = {}
    out["dft"] = np.concatenate(two(dft), 0)
    out["inv"] = np.concatenate(two(inv), 1)
    out["spec_hi"], out["spec_lo"] = two(spread @ dft)
    out["mom"] = np.concatenate(two(spread.T), 0)
    out["mom_back"] = np.concatenate(two(back.T), 0)
    out["lag_hi"], out["lag_lo"] = two(inv @ spread.T)
    out["out"] = np.concatenate(two(spread), 1)
    out["out_back"] = np.concatenate(two(back), 1)
    eye = np.eye(modes)
    out["times"] = np.kron(eye, nodes[None, :]).astype(ml_dtypes.bfloat16)
    pick = np.kron(eye, np.ones((1, NODES)))
    out["pick"] = pick.astype(ml_dtypes.bfloat16)
    return out


def mm(a, b):
    return lax.dot_general(a, b, (((1,), (0,)), ((), ())), preferred_element_type=F32)


def mm_nt(a, b):
    return lax.dot_general(a, b, (((1,), (1,)), ((), ())), preferred_element_type=F32)


def mm_tn(a, b):
    return lax.dot_general(a, b, (((0,), (0,)), ((), ())), preferred_element_type=F32)


def parts(x, count):
    out = []
    for _ in range(count):
        piece = x.astype(BF16)
        out.append(piece)
        x = x - piece.astype(F32)
    return out


def exact(op, x, table, count):
    total = None
    for piece in parts(x, count):
        term = op(piece, table)
        total = term if total is None else total + term
    return total


def powers_kernel(dec_ref, res_ref, times_ref, pick_ref, hi_ref, lo_ref, eye_ref, pow_ref, spec_ref, flat_ref):
    dec = dec_ref[...]
    modes = dec.shape[1]
    flat_ref[:modes, :] = exact(lambda x, eye: mm_nt(eye, x), dec, eye_ref[...], 3)
    flat_ref[modes:, :] = exact(lambda x, eye: mm_nt(eye, x), res_ref[...], eye_ref[...], 3)
    gain = res_ref[...] * jnp.sqrt(2.0 * dec)
    powers = jnp.exp(-exact(mm, dec, times_ref[...], 3))
    pow_ref[...] = powers
    high, low = parts(powers * exact(mm, gain, pick_ref[...], 3), 2)
    spec_ref[...] = mm(high, hi_ref[...]) + mm(low, hi_ref[...]) + mm(high, lo_ref[...])


def moved(x, halo, table):
    return mm(jnp.concatenate([x, halo.astype(BF16)], 1), table)


def weights_wide(w_ref, wide_ref):
    return mm_tn(jnp.concatenate(parts(w_ref[...], 3), 0), wide_ref[...])


def tap_sum(shifts, w, i, taps, rows):
    total = None
    for j in range(taps):
        at = (i * taps + j) * rows
        term = w[:, at : at + rows] * shifts[:, j * rows : (j + 1) * rows]
        total = term if total is None else total + term
    return total


def near_kernel(taps, q_ref, k_ref, v_ref, cot_ref, halo_ref, w_ref, pow_ref, spec_ref,
                place_ref, shift_ref, wide_ref, dft_ref, inv_ref, mom_ref, back_ref, laghi_ref, laglo_ref, pick_ref,
                qs_ref, ks_ref, vs_ref, near_ref, grad_ref, state_ref, res_ref):
    rows = q_ref.shape[1]
    halos = mm_tn(halo_ref[...], place_ref[...])
    w = weights_wide(w_ref, wide_ref)
    short = []
    for i, ref in enumerate((q_ref, k_ref, v_ref)):
        shifts = moved(ref[...], halos[:, i * rows : (i + 1) * rows], shift_ref[...])
        short.append(tap_sum(shifts, w, i, taps, rows).astype(BF16))
    qs_ref[...], ks_ref[...], vs_ref[...] = short
    gated = (short[1].astype(F32) * short[2].astype(F32)).astype(BF16)
    gmix = (cot_ref[...].astype(F32) * short[0].astype(F32)).astype(BF16)
    gated2 = jnp.concatenate([gated, gated], 1)
    gmix2 = jnp.concatenate([gmix, gmix], 1)
    z = mm(gated2, dft_ref[...])
    g = mm(gmix2, dft_ref[...])
    h = spec_ref[...]
    zr, zi = z[:, :rows], z[:, rows:]
    gr, gi = g[:, :rows], g[:, rows:]
    hr, hi = h[:, :rows], h[:, rows:]
    fwd = jnp.concatenate([zr * hr - zi * hi, zr * hi + zi * hr], 1).astype(BF16)
    bwd = jnp.concatenate([gr * hr + gi * hi, gi * hr - gr * hi], 1).astype(BF16)
    lag = jnp.concatenate([gr * zr + gi * zi, gi * zr - gr * zi], 1)
    near = mm(fwd, inv_ref[...])
    near_ref[...] = near[:, :rows] + near[:, rows:]
    grad = mm(bwd, inv_ref[...])
    grad_ref[...] = grad[:, :rows] + grad[:, rows:]
    powers = pow_ref[...]
    pick = pick_ref[...]
    state = powers * mm(gated2, back_ref[...])
    modes = pick.shape[0]

    def folded(x):
        high, low = parts(x, 2)
        return mm_nt(pick, high) + mm_nt(pick, low)

    state_ref[:modes, :] = folded(state)
    state_ref[modes:, :] = folded(powers * mm(gmix2, mom_ref[...]))
    high, low = parts(lag, 2)
    moments = mm(high, laghi_ref[...]) + mm(low, laghi_ref[...]) + mm(high, laglo_ref[...])
    res_ref[...] = folded(powers * moments)


def far_kernel(taps, q_ref, k_ref, v_ref, cot_ref, halo_ref, qs_ref, ks_ref, vs_ref,
               near_ref, grad_ref, pow_ref, all_ref, state_ref, res_ref, dec_ref, amp_ref, skip_ref,
               place_ref, shift_ref, ones_ref, out_ref, back_ref, pick_ref, sums_ref,
               mixed_ref, gq_ref, gk_ref, gv_ref, head_ref, part_ref):
    rows = q_ref.shape[1]
    modes = dec_ref.shape[0]
    dec = dec_ref[...]
    root = jnp.sqrt(2.0 * dec)
    one = jnp.exp(-dec)
    s_in = all_ref[:modes, :]
    r_in = all_ref[modes:, :]
    part_ref[:modes, :] = root * (res_ref[...] + one * s_in * state_ref[modes:, :])
    gain = amp_ref[...] * root * one
    powers = pow_ref[...]
    pick = pick_ref[...]

    def spread(x, table_ref):
        high, low = parts(powers * exact(mm_tn, x, pick, 2), 2)
        full = mm(high, table_ref[...]) + mm(low, table_ref[...])
        return full[:, :rows] + full[:, rows:]

    conv = (near_ref[...] + spread(gain * s_in, out_ref)).astype(BF16)
    gconv = (grad_ref[...] + spread(gain * r_in, back_ref)).astype(BF16)
    skip = exact(mm_tn, skip_ref[...], ones_ref[...], 3)
    qs, ks, vs = qs_ref[...].astype(F32), ks_ref[...].astype(F32), vs_ref[...].astype(F32)
    cot = cot_ref[...].astype(F32)
    gated = (ks * vs).astype(BF16).astype(F32)
    gmix = (cot * qs).astype(BF16).astype(F32)
    mix = conv.astype(F32) + skip * gated
    mixed_ref[...] = (qs * mix).astype(BF16)
    gq = (cot * mix).astype(BF16)
    ggated = gconv.astype(F32) + skip * gmix
    gk = (ggated * vs).astype(BF16)
    gv = (ggated * ks).astype(BF16)
    gq_ref[...], gk_ref[...], gv_ref[...] = gq, gk, gv
    first = (lax.broadcasted_iota(jnp.int32, (8, rows), 0) == lax.broadcasted_iota(jnp.int32, (8, rows), 1)).astype(BF16)
    head_ref[...] = jnp.concatenate([mm_nt(first, x) for x in (gq, gk, gv)], 0).astype(BF16)
    halos = mm_tn(halo_ref[...], place_ref[...])
    products = []
    for i, (ref, grads) in enumerate(((q_ref, gq), (k_ref, gk), (v_ref, gv))):
        values = grads.astype(F32)
        shifts = moved(ref[...], halos[:, i * rows : (i + 1) * rows], shift_ref[...])
        for j in range(taps):
            products.append((values * shifts[:, j * rows : (j + 1) * rows]).astype(BF16))
    products.append((gmix * gated).astype(BF16))
    sums = mm(jnp.concatenate(products, 1), sums_ref[...])
    part_ref[modes:, :] = sums.T[:32, :]


def anti_taps(taps, grads, halo, w, place_ref, shift_ref, wide_ref):
    rows = grads[0].shape[1]
    halos = mm_tn(halo, place_ref[...])
    w = mm_tn(jnp.concatenate(parts(w, 3), 0), wide_ref[...])
    outs = []
    for i, x in enumerate(grads):
        shifts = moved(x, halos[:, i * rows : (i + 1) * rows], shift_ref[...])
        outs.append(tap_sum(shifts, w, i, taps, rows).astype(BF16))
    return outs


def last_kernel(taps, gq_ref, gk_ref, gv_ref, halo_ref, w_ref, place_ref, shift_ref, wide_ref, oq_ref, ok_ref, ov_ref):
    oq_ref[...], ok_ref[...], ov_ref[...] = anti_taps(
        taps, (gq_ref[...], gk_ref[...], gv_ref[...]), halo_ref[...], w_ref[...], place_ref, shift_ref, wide_ref)


def partners(axis):
    n = lax.axis_size(axis)
    me = lax.axis_index(axis)
    barrier = pltpu.get_barrier_semaphore()
    where = [lax.rem(me + d, n) for d in range(n)]
    for d in range(1, n):
        pl.semaphore_signal(barrier, inc=1, device_id={axis: where[d]}, device_id_type=pl.DeviceIdType.MESH)
    pl.semaphore_wait(barrier, n - 1)
    return n, me, where


def send(src, dst, send_sem, recv_sem, axis, target):
    copy = pltpu.make_async_remote_copy(
        src_ref=src, dst_ref=dst, send_sem=send_sem, recv_sem=recv_sem,
        device_id={axis: target}, device_id_type=pl.DeviceIdType.MESH)
    copy.start()
    return copy


def first_kernel(dec_ref, res_ref, times_ref, pick_ref, hi_ref, lo_ref, eye_ref, q_ref, k_ref, v_ref,
                 pow_ref, spec_ref, flat_ref, halo_ref, tails, got, sems):
    rows = q_ref.shape[1]
    n = lax.axis_size("ctx")
    me = lax.axis_index("ctx")
    right, left = lax.rem(me + 1, n), lax.rem(me + n - 1, n)
    copy = pltpu.make_async_remote_copy(
        src_ref=tails, dst_ref=got, send_sem=sems.at[0], recv_sem=sems.at[1],
        device_id={"ctx": right}, device_id_type=pl.DeviceIdType.MESH)

    @pl.when(pl.program_id(0) == 0)
    def _():
        barrier = pltpu.get_barrier_semaphore()
        for other in (right, left):
            pl.semaphore_signal(barrier, inc=1, device_id={"ctx": other}, device_id_type=pl.DeviceIdType.MESH)
        shape = (8, rows)
        last = (lax.broadcasted_iota(jnp.int32, shape, 0) + (rows - 8) == lax.broadcasted_iota(jnp.int32, shape, 1)).astype(BF16)
        tails[...] = jnp.concatenate([mm_nt(last, ref[...]) for ref in (q_ref, k_ref, v_ref)], 0).astype(BF16)
        pl.semaphore_wait(barrier, 2)
        copy.start()

    powers_kernel(dec_ref, res_ref, times_ref, pick_ref, hi_ref, lo_ref, eye_ref, pow_ref, spec_ref, flat_ref)

    @pl.when(pl.program_id(0) == pl.num_programs(0) - 1)
    def _():
        copy.wait()
        halo_ref[...] = jnp.where(me > 0, got[...].astype(F32), 0.0).astype(BF16)


def gather_kernel(rows, state_ref, dec_ref, in_ref, out, got, send_sem, recv_sem):
    modes = dec_ref.shape[0] // 2
    out[0] = state_ref[:modes, :].astype(BF16)
    out[1] = state_ref[modes:, :].astype(BF16)
    n, me, where = partners("ctx")
    copies = []
    for d in range(1, n):
        kind = jnp.where(where[d] > me, 0, 1)
        copies.append(send(out.at[kind], got.at[d], send_sem.at[d], recv_sem.at[d], "ctx", where[d]))
    chunk = jnp.exp(-dec_ref[:modes, :] * float(rows))
    for copy in copies:
        copy.wait()
    s = jnp.zeros(chunk.shape, F32)
    for d in range(n - 1, 0, -1):
        s = jnp.where(me >= d, s * chunk + got[d].astype(F32), s)
    in_ref[:modes, :] = s
    r = jnp.zeros(chunk.shape, F32)
    for d in range(1, n):
        r = jnp.where(me < d, r * chunk + got[d].astype(F32), r)
    in_ref[modes:, :] = r


def reduce_kernel(scale, taps, block, part_ref, head_ref, gq_ref, gk_ref, gv_ref, w_ref, place_ref, shift_ref, wide_ref,
                  total_ref, oq_ref, ok_ref, ov_ref, parted, got, mine, full, heads, ends, send_sem, recv_sem, back_send, back_recv, halo_sem):
    n = lax.axis_size("ctx")
    width = parted.shape[2]
    for p in range(n):
        parted[p] = part_ref[:, p * width : (p + 1) * width].astype(BF16)
    n, me, where = partners("ctx")
    halo = send(head_ref, heads, halo_sem.at[0], halo_sem.at[1], "ctx", where[n - 1])
    copies = []
    for d in range(1, n):
        copies.append(send(parted.at[where[d]], got.at[d], send_sem.at[d], recv_sem.at[d], "ctx", where[d]))
    halo.wait()
    ends[...] = jnp.where(me < n - 1, heads[...].astype(F32), 0.0).astype(BF16)
    count = gq_ref.shape[0] // block

    def step(b, carry):
        at = pl.ds(pl.multiple_of(b * block, block), block)
        oq_ref[at, :], ok_ref[at, :], ov_ref[at, :] = anti_taps(
            taps, (gq_ref[at, :], gk_ref[at, :], gv_ref[at, :]), ends[:, at], w_ref[:, at], place_ref, shift_ref, wide_ref)
        return carry

    lax.fori_loop(0, count // 2, step, 0)
    total = parted[me].astype(F32)
    for d in range(1, n):
        copies[d - 1].wait()
        total = total + got[d].astype(F32)
    mine[...] = (total * scale).astype(BF16)
    copies = []
    for d in range(1, n):
        copies.append(send(mine, full.at[d], back_send.at[d], back_recv.at[d], "ctx", where[d]))
    full[0] = mine[...]
    lax.fori_loop(count // 2, count, step, 0)
    for copy in copies:
        copy.wait()
    for p in range(n):
        total_ref[:, p * width : (p + 1) * width] = full[lax.rem(me - p + n, n)].astype(F32)


def passed_along(block, axis, distance):
    devices = range(lax.axis_size(axis))
    route = [(i - distance, i) for i in devices if i - distance in devices]
    return lax.ppermute(block, axis, route)


def per_device(
    queries, key_signal, value_signal, cotangent, short_weight, residues, decay_rates, skip_gain
):
    channels, rows = queries.shape
    taps = short_weight.shape[1]
    modes = residues.shape[1]
    devices = lax.axis_size("ctx")
    block = min(256, channels)
    grid = (channels // block,)
    tab = {name: jnp.asarray(value) for name, value in tables(rows, modes).items()}
    wide = modes * NODES
    tail = np.zeros((24, 3 * rows), np.float32)
    head = np.zeros((24, 3 * rows), np.float32)
    for i in range(3):
        for j in range(8):
            tail[i * 8 + j, i * rows + rows - 8 + j] = 1
            head[i * 8 + j, i * rows + j] = 1
    tail, head = jnp.asarray(tail, BF16), jnp.asarray(head, BF16)
    sums = np.zeros(((3 * taps + 1) * rows, 128), np.float32)
    for i in range(3 * taps + 1):
        sums[i * rows : (i + 1) * rows, i] = 1
    sums = jnp.asarray(sums, BF16)

    def tall(width):
        return pl.BlockSpec((block, width), lambda i: (i, 0))

    def flat(height):
        return pl.BlockSpec((height, block), lambda i: (0, i))

    def whole(x):
        return pl.BlockSpec(x.shape, lambda i: (0,) * x.ndim)

    def shape(*dims, kind=F32):
        return jax.ShapeDtypeStruct(dims, kind)

    params = pltpu.CompilerParams(vmem_limit_bytes=60 * 1024 * 1024)
    dma = pltpu.SemaphoreType.DMA
    vmem = pl.BlockSpec(memory_space=pltpu.VMEM)
    w_flat = jnp.concatenate([short_weight.reshape(3 * taps, channels), jnp.zeros((24 - 3 * taps, channels), F32)], 0)
    skip = skip_gain[None, :]
    both = [np.zeros((2 * rows, taps * rows), np.float32) for _ in range(2)]
    for j in range(taps):
        for t in range(rows):
            both[0][t - j if t >= j else 2 * rows + t - j, j * rows + t] = 1
            both[1][t + j, j * rows + t] = 1
    before, after = (jnp.asarray(x, BF16) for x in both)
    spread_w = np.zeros((24, 3 * taps * rows), np.float32)
    for i in range(3 * taps):
        spread_w[i, i * rows : (i + 1) * rows] = 1
    spread_w = jnp.asarray(np.tile(spread_w, (3, 1)), BF16)

    args = (tab["times"], tab["pick"], tab["spec_hi"], tab["spec_lo"], jnp.eye(modes, dtype=BF16), queries, key_signal, value_signal)
    powers, spec, flats, left = pl.pallas_call(
        first_kernel,
        grid=grid,
        in_specs=[tall(modes), tall(modes)] + [whole(x) for x in args],
        out_specs=[tall(wide), tall(2 * rows), flat(2 * modes), pl.BlockSpec((24, channels), lambda i: (0, 0))],
        out_shape=[shape(channels, wide), shape(channels, 2 * rows), shape(2 * modes, channels), shape(24, channels, kind=BF16)],
        scratch_shapes=[pltpu.VMEM((24, channels), BF16)] * 2 + [dma((2,))],
        compiler_params=pltpu.CompilerParams(collective_id=2, has_side_effects=True, vmem_limit_bytes=60 * 1024 * 1024),
        cost_estimate=pl.CostEstimate(flops=10**9, bytes_accessed=5 * 10**6, transcendentals=10**6),
        name="powers",
    )(decay_rates, residues, *args)

    args = (tail, before, spread_w, tab["dft"], tab["inv"], tab["mom"], tab["mom_back"], tab["lag_hi"], tab["lag_lo"], tab["pick"])
    q_short, k_short, v_short, near, grad, state, res = pl.pallas_call(
        functools.partial(near_kernel, taps),
        grid=grid,
        in_specs=[tall(rows)] * 4 + [flat(24), flat(24), tall(wide), tall(2 * rows)] + [whole(x) for x in args],
        out_specs=[tall(rows)] * 5 + [flat(2 * modes), flat(modes)],
        out_shape=[shape(channels, rows, kind=BF16)] * 3 + [shape(channels, rows)] * 2 + [shape(2 * modes, channels), shape(modes, channels)],
        compiler_params=params,
        name="near",
    )(queries, key_signal, value_signal, cotangent, left, w_flat, powers, spec, *args)

    every = pl.pallas_call(
        functools.partial(gather_kernel, rows),
        in_specs=[vmem] * 2,
        out_specs=vmem,
        out_shape=shape(2 * modes, channels),
        scratch_shapes=[
            pltpu.VMEM((2, modes, channels), BF16), pltpu.VMEM((devices, modes, channels), BF16),
            dma((devices,)), dma((devices,)),
        ],
        compiler_params=pltpu.CompilerParams(collective_id=0, has_side_effects=True, vmem_limit_bytes=60 * 1024 * 1024),
        name="gather",
    )(state, flats)
    args = (tail, before, jnp.ones((1, rows), BF16), tab["out"], tab["out_back"], tab["pick"], sums)
    mixed, gq, gk, gv, heads, part = pl.pallas_call(
        functools.partial(far_kernel, taps),
        grid=grid,
        in_specs=[tall(rows)] * 4 + [flat(24)] + [tall(rows)] * 5
        + [tall(wide), flat(2 * modes), flat(2 * modes), flat(modes), flat(modes), pl.BlockSpec((modes, block), lambda i: (1, i)), flat(1)]
        + [whole(x) for x in args],
        out_specs=[tall(rows)] * 4 + [flat(24), flat(modes + 32)],
        out_shape=[shape(channels, rows, kind=BF16)] * 4 + [shape(24, channels, kind=BF16), shape(modes + 32, channels)],
        compiler_params=params,
        name="far",
    )(queries, key_signal, value_signal, cotangent, left, q_short, k_short, v_short, near, grad,
      powers, every, state, res, flats, flats, skip, *args)

    scale = 1.0 / math.sqrt(rows * devices)
    width = channels // devices
    if width % 128 == 0:
        height = modes + 32
        totals, *grads = pl.pallas_call(
            functools.partial(reduce_kernel, scale, taps, block),
            in_specs=[vmem] * 9,
            out_specs=[vmem] * 4,
            out_shape=[shape(height, channels)] + [shape(channels, rows, kind=BF16)] * 3,
            scratch_shapes=[
                pltpu.VMEM((devices, height, width), BF16), pltpu.VMEM((devices, height, width), BF16),
                pltpu.VMEM((height, width), BF16), pltpu.VMEM((devices, height, width), BF16),
                pltpu.VMEM((24, channels), BF16), pltpu.VMEM((24, channels), BF16),
                dma((devices,)), dma((devices,)), dma((devices,)), dma((devices,)), dma((2,)),
            ],
            compiler_params=pltpu.CompilerParams(collective_id=1, has_side_effects=True, vmem_limit_bytes=60 * 1024 * 1024),
            name="reduce",
        )(part, heads, gq, gk, gv, w_flat, head, after, spread_w)
    else:
        right = passed_along(heads, "ctx", -1)
        totals = lax.psum(part, "ctx") * scale
        grads = pl.pallas_call(
            functools.partial(last_kernel, taps),
            grid=grid,
            in_specs=[tall(rows)] * 3 + [flat(24), flat(24), whole(head), whole(after), whole(spread_w)],
            out_specs=[tall(rows)] * 3,
            out_shape=[shape(channels, rows, kind=BF16)] * 3,
            compiler_params=params,
            cost_estimate=pl.CostEstimate(flops=10**9, bytes_accessed=5 * 10**6, transcendentals=0),
            name="last",
        )(gq, gk, gv, right, w_flat, head, after, spread_w)
    return (
        mixed,
        *grads,
        totals[modes : modes + 3 * taps].reshape(3, taps, channels),
        totals[:modes].T,
        totals[modes + 3 * taps],
    )


def solution(mesh):
    signal = P("tp", "ctx")
    in_specs = (signal,) * 4 + (P(None, None, "tp"), P("tp", None), P("tp", None), P("tp"))
    out_specs = (signal,) * 4 + (P(None, None, "tp"), P("tp", None), P("tp"))
    return jax.shard_map(
        per_device, mesh=mesh, in_specs=in_specs, out_specs=out_specs, check_vma=False
    )
```
